256 devices in a mesh: rep: 32 (over z, y), ch: 8 (over x, core).
Axes of the slice: x: 4, y: 4, z: 8, core: 2. Of those that a mesh axis runs over, the one named last changes fastest.
Arguments:
- patches: bfloat16 [32, 768, 4352], P('rep', 'ch'), may hold values from -28 to 28
- cotangents: bfloat16 [32, 768, 2688], P('rep', 'ch'), may hold values from -0.06 to 0.06
- weight: float32 [768, 27, 768], P(('ch', 'rep')), may hold values from -0.0390625 to 0.0390625
- momentum: float32 [768, 27, 768], P(('ch', 'rep')), may hold values from -6 to 6
Outputs:
- new_weight: float32 [768, 27, 768], P(('ch', 'rep'))
- new_momentum: float32 [768, 27, 768], P(('ch', 'rep'))
The draws below stay inside these ranges and needn't reach their ends.
All inputs are finite; a program needn't handle non-finite values.
Results may differ from the reference program's by a relative error of at most 0.0003.
Values may be sent and summed in bfloat16 or wider, within the bound.
A program may use at most 128 MiB of HBM per device.

```python
import math
import jax
import jax.numpy as jnp
from jax import lax

C_IN = 768
C_OUT = 768
KERNEL = 3
DEPTH = 6
HEIGHT = 14
WIDTH = 32
VOX = 2688
TAPS = 27
LEVELS = 5
N_REP = 32
N_CH = 8


def draw_patches(key, part):
    span_cells = (DEPTH + KERNEL - 1) * (HEIGHT + KERNEL - 1) * (WIDTH + KERNEL - 1)
    shape_one = (1, C_IN, span_cells)
    full_shape = (N_REP, C_IN, span_cells)
    common = jnp.clip(jax.random.normal(jax.random.fold_in(key, 11), shape_one, jnp.float32), -4.0, 4.0)
    own_part = jnp.clip(jax.random.normal(jax.random.fold_in(key, 12), full_shape, jnp.float32), -4.0, 4.0)
    shared = 0.8
    scales = jnp.exp(jax.random.uniform(jax.random.fold_in(key, 13), (C_IN,), jnp.float32, math.log(0.5), math.log(5.0)))
    values = scales[None, :, None] * (shared * common + math.sqrt(1.0 - shared * shared) * own_part)
    return values.astype(jnp.bfloat16)


def draw_cotangents(key, part):
    voxels = DEPTH * HEIGHT * WIDTH
    shape_one = (1, C_OUT, voxels)
    full_shape = (N_REP, C_OUT, voxels)
    common = jnp.clip(jax.random.normal(jax.random.fold_in(key, 21), shape_one, jnp.float32), -4.0, 4.0)
    own_part = jnp.clip(jax.random.normal(jax.random.fold_in(key, 22), full_shape, jnp.float32), -4.0, 4.0)
    local_count = C_OUT // N_CH
    channel_ids = jnp.arange(C_OUT)
    position = (channel_ids % local_count).astype(jnp.float32) / max(local_count - 1, 1)
    ramp = channel_ids.astype(jnp.float32) / max(C_OUT - 1, 1)
    jitter = jax.random.uniform(jax.random.fold_in(key, 23), (C_OUT,), jnp.float32, -0.05, 0.05)
    shared = (0.3 + 0.6 * jnp.abs(2.0 * position - 1.0) + jitter)[None, :, None]
    slope_jitter = jax.random.uniform(jax.random.fold_in(key, 25), (C_OUT,), jnp.float32, -0.2, 0.2)
    direction = 2.0 * (2.0 * position - 1.0) + slope_jitter
    replica_pos = jnp.arange(N_REP).astype(jnp.float32) / max(N_REP - 1, 1) - 0.5
    replica_scale = jnp.exp(math.log(3.0) * replica_pos[:, None] * direction[None, :])
    channel_scale = (1.0 + 2.0 * ramp) * jnp.exp(jax.random.uniform(jax.random.fold_in(key, 24), (C_OUT,), jnp.float32, 0.0, math.log(2.0)))
    values = 0.0005 * replica_scale[:, :, None] * channel_scale[None, :, None] * (shared * common + jnp.sqrt(1.0 - shared * shared) * own_part)
    return values.astype(jnp.bfloat16)


def shard_levels(rng, extent, split, least, top_value):
    level, own = 1.0, jax.random.fold_in(rng, 6)
    for dim, shards_of in split:
        heights = jnp.exp(jax.random.uniform(jax.random.fold_in(own, dim), (shards_of,), jnp.float32, least / len(split), top_value / len(split)))
        level = level * jnp.repeat(heights, extent[dim] // shards_of).reshape([-1 if axis == dim else 1 for axis in range(len(extent))])
    return level


def normal_values(stream_key, shape, spread, bound, cuts=(), kind=jnp.bfloat16):
    gain = shard_levels(stream_key, shape, cuts, -0.22, 0.18) if cuts else 1.0
    result = jax.random.normal(stream_key, shape, jnp.float32) * spread * gain
    return jnp.minimum(jnp.maximum(result, -bound), bound).astype(kind)


def setup_inputs(seed: int = 0) -> dict:
    splits = jax.random.split(jax.random.key(seed), 5)
    return {
        "patches": draw_patches(jax.random.fold_in(splits[4], 71), 0),
        "cotangents": draw_cotangents(jax.random.fold_in(splits[4], 71), 0),
        "weight": normal_values(splits[2], (C_OUT, TAPS, C_IN), (TAPS * C_IN) ** -0.5, 0.0390625, ((0, 256),), jnp.float32),
        "momentum": normal_values(splits[3], (C_OUT, TAPS, C_IN), 1.0, 6.0, ((0, 256),), jnp.float32),
    }


momentum_decay = 0.9
learning_rate = 0.05

def replica_gradient(patch, cotangent):
    flat_cot = cotangent.astype(jnp.float32)
    volume = patch.reshape(C_IN, DEPTH + KERNEL - 1, HEIGHT + KERNEL - 1, WIDTH + KERNEL - 1)

    def one_tap(tap_index):
        first_off = tap_index // (KERNEL * KERNEL)
        second_off = tap_index // KERNEL % KERNEL
        third_off = tap_index % KERNEL
        window = lax.dynamic_slice(volume, (jnp.int32(0), first_off, second_off, third_off), (C_IN, DEPTH, HEIGHT, WIDTH))
        window = window.astype(jnp.float32).reshape(C_IN, VOX)
        return jnp.dot(flat_cot, window.T, precision=lax.Precision.HIGHEST, preferred_element_type=jnp.float32)
    per_tap = lax.map(one_tap, jnp.arange(TAPS, dtype=jnp.int32))
    return jnp.transpose(per_tap, (1, 0, 2))

def adasum_pair(former, latter):
    inner = jnp.sum(former * latter)
    former_sq = jnp.sum(former * former)
    latter_sq = jnp.sum(latter * latter)
    return (1.0 - inner / (2.0 * former_sq)) * former + (1.0 - inner / (2.0 * latter_sq)) * latter

def reference(patches, cotangents, weight, momentum):

    def leaf_grad(replica):
        return replica_gradient(patches[replica], cotangents[replica])

    def combine(low_bits, depth_bits):
        if depth_bits == LEVELS:
            return leaf_grad(low_bits)
        return adasum_pair(combine(low_bits, depth_bits + 1), combine(low_bits + 2 ** depth_bits, depth_bits + 1))
    combined = combine(0, 0)
    new_momentum = momentum_decay * momentum + combined
    new_weight = weight - learning_rate * new_momentum
    return (new_weight, new_momentum)
```

```python
import jax
import jax.numpy as jnp
from jax import lax
from jax.experimental import pallas as pl
from jax.experimental.pallas import tpu as pltpu
from jax.sharding import PartitionSpec as P

KERNEL = 3
DEPTH = 6
HEIGHT = 14
WIDTH = 32
ROW = WIDTH + KERNEL - 1
PLANE = (HEIGHT + KERNEL - 1) * ROW
CELLS = (DEPTH + KERNEL - 1) * PLANE
VOX = DEPTH * HEIGHT * WIDTH

Z = 8
Y = 4
Z_GROUPS = [[4 * z + y for z in range(Z)] for y in range(Y)]
Y_GROUPS = [[4 * z + y for y in range(Y)] for z in range(Z)]

momentum_decay = 0.9
learning_rate = 0.05


def grads_kernel(d_ref, p_ref, g_ref, k_ref, s_ref, ps_ref):
    r = pl.program_id(0)

    @pl.when(r == 0)
    def _():
        s_ref[...] = jnp.zeros_like(s_ref)

    for i in range(DEPTH):
        for j in range(HEIGHT):
            src = d_ref[0, :, pl.ds((i * HEIGHT + j) * WIDTH, WIDTH)]
            for a in range(KERNEL):
                s_ref[a * 96 : (a + 1) * 96, pl.ds((a + i) * PLANE + j * ROW, WIDTH)] = src
    for b in range(KERNEL):
        for e in range(KERNEL):
            s = ROW * b + e
            row = (b * KERNEL + e) * 96
            if s == 0:
                ps_ref[row : row + 96, :] = p_ref[0]
            else:
                ps_ref[row : row + 96, : CELLS - s] = p_ref[0, :, s:]
                ps_ref[row : row + 96, CELLS - s :] = jnp.zeros((96, s), jnp.bfloat16)
    g_ref[r] = lax.dot_general(
        s_ref[...], ps_ref[...], (((1,), (1,)), ((), ())), preferred_element_type=jnp.float32
    )
    for q in range(Z):

        @pl.when(q <= r)
        def _():
            k_ref[r, q] = jnp.sum(g_ref[r] * g_ref[q])

        @pl.when(q > r)
        def _():
            k_ref[r, q] = 0.0


def grads(d, p):
    return pl.pallas_call(
        grads_kernel,
        grid=(Z,),
        in_specs=[
            pl.BlockSpec((1, 96, VOX), lambda r: (r, 0, 0)),
            pl.BlockSpec((1, 96, CELLS), lambda r: (r, 0, 0)),
        ],
        out_specs=[
            pl.BlockSpec((Z, 288, 864), lambda r: (0, 0, 0), pipeline_mode=pl.Buffered(1)),
            pl.BlockSpec(memory_space=pltpu.SMEM),
        ],
        out_shape=[
            jax.ShapeDtypeStruct((Z, 288, 864), jnp.float32),
            jax.ShapeDtypeStruct((Z, Z), jnp.float32),
        ],
        scratch_shapes=[
            pltpu.VMEM((288, CELLS), jnp.bfloat16),
            pltpu.VMEM((864, CELLS), jnp.bfloat16),
        ],
        compiler_params=pltpu.CompilerParams(vmem_limit_bytes=56 * 2**20),
    )(d, p)


def tree_weights(gram):
    n = gram.shape[0]
    coef = jnp.eye(n, dtype=jnp.float32)
    while n > 1:
        n //= 2
        lo, hi = coef[:n], coef[n:]
        gram_hi = jnp.sum(hi[:, :, None] * gram[None], axis=1)
        gram_lo = jnp.sum(lo[:, :, None] * gram[None], axis=1)
        inner = jnp.sum(lo * gram_hi, axis=1)
        lo_sq = jnp.sum(lo * gram_lo, axis=1)
        hi_sq = jnp.sum(hi * gram_hi, axis=1)
        coef = (1.0 - inner / (2.0 * lo_sq))[:, None] * lo + (1.0 - inner / (2.0 * hi_sq))[:, None] * hi
    return coef[0]


def shards(patches, cotangents, weight, momentum):
    d = cotangents[0].reshape(Z, Y, 3, VOX).transpose(1, 0, 2, 3).reshape(96, VOX)
    d = lax.all_gather(d, "rep", axis_index_groups=Z_GROUPS)
    p = patches[0].reshape(Z, 12, CELLS)
    p = lax.all_to_all(p, "rep", 0, 0, axis_index_groups=Z_GROUPS, tiled=True)
    p = lax.all_gather(p, "ch", axis=1, tiled=True)
    g, gram = grads(d, p)
    gram = lax.psum(lax.psum(gram, "ch"), "rep", axis_index_groups=Z_GROUPS)
    gram = gram + jnp.tril(gram, -1).T
    w = tree_weights(gram)
    v = jnp.sum(w[:, None, None] * g, axis=0)
    v = v.reshape(KERNEL, Y, 24, 864)
    v = lax.all_to_all(v, "rep", 1, 0, axis_index_groups=Y_GROUPS)
    gram = jnp.stack([jnp.stack([jnp.sum(v[i] * v[j]) for j in range(Y)]) for i in range(Y)])
    gram = lax.psum(gram, ("rep", "ch"))
    w = tree_weights(gram)
    v = jnp.sum(w[:, None, None, None] * v, axis=0)
    v = v.reshape(KERNEL, Z, 3, 864)
    v = lax.all_to_all(v, "rep", 1, 0, axis_index_groups=Z_GROUPS)
    v = v.reshape(Z, KERNEL, 3, 9, 8, 12).transpose(2, 1, 3, 4, 0, 5).reshape(weight.shape)
    new_momentum = momentum_decay * momentum + v
    new_weight = weight - learning_rate * new_momentum
    return (new_weight, new_momentum)


def solution(mesh):
    in_specs = (
        P("rep", "ch", None),
        P("rep", "ch", None),
        P(("ch", "rep"), None, None),
        P(("ch", "rep"), None, None),
    )
    out_specs = (P(("ch", "rep"), None, None), P(("ch", "rep"), None, None))
    return jax.shard_map(shards, mesh=mesh, in_specs=in_specs, out_specs=out_specs, check_vma=False)
```
